32 devices in a mesh: ep: 2 (over core), dp: 16 (over z, y, x).
Axes of the slice: x: 2, y: 2, z: 4, core: 2. Of those that a mesh axis runs over, the one named last changes fastest.
Arguments:
- tokens: bfloat16 [512, 7168], P('dp', 'ep'), may hold values from -6 to 6
- gate_weight: bfloat16 [16, 7168, 1024], P('dp', 'ep'), may hold values from -0.0625 to 0.0625
- up_weight: bfloat16 [16, 7168, 1024], P('dp', 'ep'), may hold values from -0.0625 to 0.0625
- down_weight: bfloat16 [16, 1024, 7168], P('dp', None, 'ep'), may hold values from -0.1875 to 0.1875
- targets: int32 [512, 8], P('dp'), may hold values from 0 to 15, all different within a row; in each aligned block of 32 rows (0 to 31, 32 to 63, ...) at most 32 rows name the same one
- mixing: float32 [512, 8], P('dp'), may hold values from 0.05 to 1
- move_plan: int32 [16], replicated, may hold values from 0 to 15, as said below
Outputs:
- mixed: bfloat16 [512, 7168], P('dp', 'ep')
The draws below stay inside these ranges and needn't reach their ends.
Inputs may be any that keep to these rules, and one draw needn't show every extreme that they name: `targets`: each row names 8 different slots; within the 32 rows of one token group no slot is named more than 32 times, and in some groups one slot exactly 32 times. `move_plan`: every entry is either its own slot or one common source slot; the source serves its own copy; the slot after the source and the slot half of 16 after it (cyclically) always serve the source's copy, and each other slot does so with probability one half.
All inputs are finite; a program needn't handle non-finite values.
Results may differ from the reference program's by a relative error of at most 0.0058.
Values may be sent and summed in bfloat16 or wider, within the bound.
A program may use at most 128 MiB of HBM per device.

```python
import math
import jax
import jax.numpy as jnp
import numpy as np
from jax import lax

D = 7168
FF = 1024
TOP = 8
TOK_G = 32
CAP = 32
TOKENS = 512
N_EP = 2
N_DP = 16


def draw_move_plan(key, part):
    first, second = jax.random.split(jax.random.fold_in(key, 7))
    source_slot = jax.random.randint(first, (), 0, N_DP)
    slots_all = jnp.arange(N_DP, dtype=jnp.int32)
    offset = (slots_all - source_slot) % N_DP
    coins = jax.random.randint(second, (N_DP,), 0, 2)
    served = (offset != 0) & ((coins == 1) | (offset == 1) | (offset == N_DP // 2))
    return jnp.where(served, source_slot, slots_all).astype(jnp.int32)


def steps_of(rng, extent, cuts, smallest, largest):
    factor_of = 1.0
    for position, blocks in cuts:
        draws = jax.random.uniform(jax.random.fold_in(jax.random.fold_in(rng, 6), position), (blocks,), jnp.float32, smallest / len(cuts), largest / len(cuts))
        factor_of = factor_of * jnp.repeat(jnp.exp(draws), extent[position] // blocks).reshape((-1,) + (1,) * (len(extent) - 1 - position))
    return factor_of


def assign_block(stream_key, own, number, rows, count, top, bound, slope):
    ranking = jax.random.permutation(stream_key, count)
    crowded, ordinary = load_shares(count, rows * top, bound, slope, True), load_shares(count, rows * top, bound, slope, False)
    places = jnp.arange(count)

    def named(lengths, turn):
        used = int((lengths > 0).sum())
        fixed = max(1, used // 4)
        passed = fixed + (places - fixed + turn * (used - fixed)) % max(1, count - fixed)
        return jnp.zeros((count,), jnp.int32).at[ranking[jnp.where(places < fixed, places, passed)]].set(jnp.asarray(lengths, jnp.int32))

    lengths = jnp.where(number % 4 == 0, named(crowded, number // 4), named(ordinary, number - number // 4 - 1))
    mixed = jax.random.permutation(jax.random.fold_in(own, 3), count)
    giver, receiver = mixed[0:count // 2 * 2:2], mixed[1:count // 2 * 2:2]
    slack = jnp.minimum(lengths[giver] - 1, bound - lengths[receiver]) // 2
    slack = jnp.where((giver == ranking[0]) | (receiver == ranking[0]) | (lengths[receiver] == 0), 0, jnp.maximum(slack, 0))
    passed = jax.random.randint(jax.random.fold_in(own, 4), (count // 2,), 0, 1 << 20) % (slack + 1)
    lengths = lengths.at[giver].add(-passed).at[receiver].add(passed)
    labels = jnp.searchsorted(jnp.cumsum(lengths), jnp.arange(rows * top), side="right").astype(jnp.int32)
    listing = labels.reshape(top, rows).T
    listing = listing[jax.random.permutation(jax.random.fold_in(own, 1), rows)]
    turn = jax.random.randint(jax.random.fold_in(own, 2), (rows, 1), 0, top)
    return jnp.take_along_axis(listing, (jnp.arange(top)[None, :] + turn) % top, axis=1)


def load_shares(amount, total, reach, slope, full):
    portions = [(1 << 20) // math.isqrt(rank ** slope) + 1 for rank in range(1, amount + 1)]
    largest = reach if full else min(reach, max(-(-total // amount), total * portions[0] // sum(portions)))
    least = 1 if total - largest >= amount - 1 else 0
    given, surplus = [largest] + [least] * (amount - 1), total - largest - least * (amount - 1)
    while surplus > 0:
        free = [i for i in range(1, amount) if given[i] < largest] or [i for i in range(1, amount) if given[i] < reach]
        whole, remaining = sum([portions[i] for i in free]), surplus
        for i in free:
            addition = min(reach - given[i], max(1, remaining * portions[i] // whole), surplus)
            given[i] = given[i] + addition
            surplus = surplus - addition
    return np.array(given)


def bell_draw(rng, shape, deviation, reach, shards=(), held_as=jnp.bfloat16):
    array = jax.random.normal(rng, shape, jnp.float32) * deviation
    if len(shards) > 0:
        array = steps_of(rng, shape, shards, -0.22, 0.18) * array
    return jnp.clip(array, min=-reach, max=reach).astype(held_as)


def setup_inputs(seed: int = 0) -> dict:
    streams_of = jax.random.split(jax.random.key(seed), 8)
    tokens = bell_draw(streams_of[0], (TOKENS, D), 1.0, 6.0, ((0, 16), (1, 2)))
    gate_weight = bell_draw(streams_of[1], (N_DP, D, FF), D ** -0.5, 0.0625, ((0, 16), (1, 2)))
    up_weight = bell_draw(streams_of[2], (N_DP, D, FF), D ** -0.5, 0.0625, ((0, 16), (1, 2)))
    down_weight = bell_draw(streams_of[3], (N_DP, FF, D), FF ** -0.5, 0.1875, ((0, 16), (2, 2)))
    targets_keys = jax.random.split(jax.random.fold_in(streams_of[4], 1), TOKENS // TOK_G)
    targets_turns = jax.random.permutation(jax.random.fold_in(streams_of[4], 3), TOKENS // TOK_G)
    targets = jax.vmap(lambda own, number: assign_block(jax.random.fold_in(streams_of[4], 2), own, number, TOK_G, N_DP, TOP, CAP, 2))(targets_keys, targets_turns).reshape((TOKENS, TOP))
    mixing = jnp.clip(jnp.exp(math.log(1.0) - 2.9957323 * jax.random.uniform(streams_of[5], (TOKENS, TOP), jnp.float32) ** steps_of(streams_of[5], (TOKENS, TOP), ((0, 16),), -0.2, 0.2)), 0.05, 1.0)
    move_plan = draw_move_plan(jax.random.fold_in(streams_of[7], 71), 0)
    return dict(tokens=tokens, gate_weight=gate_weight, up_weight=up_weight, down_weight=down_weight, targets=targets, mixing=mixing, move_plan=move_plan)


def run_expert(rows, gate_cols, up_cols, down_rows):
    count = rows.shape[0]
    width = D // N_EP
    blocks = rows.reshape(count, N_EP, width).astype(jnp.float32)
    gate_blocks = gate_cols.reshape(N_EP, width, FF).astype(jnp.float32)
    up_blocks = up_cols.reshape(N_EP, width, FF).astype(jnp.float32)
    gate = jnp.einsum("nbd,bdf->nf", blocks, gate_blocks)
    up = jnp.einsum("nbd,bdf->nf", blocks, up_blocks)
    hidden = (jax.nn.silu(gate) * up).astype(jnp.bfloat16)
    return jnp.dot(hidden, down_rows, preferred_element_type=jnp.float32).astype(jnp.bfloat16)


def reference(tokens, gate_weight, up_weight, down_weight, targets, mixing, move_plan):
    flat_targets = targets.reshape(-1).astype(jnp.int32)
    flat_mixing = mixing.reshape(-1)
    slots = N_DP * CAP
    places = jnp.arange(slots, dtype=jnp.int32)
    plan = move_plan.astype(jnp.int32)

    def visit(total, group):
        anchor = plan[group].astype(jnp.int32)
        gate_cols = lax.dynamic_index_in_dim(gate_weight, anchor, 0, keepdims=False)
        up_cols = lax.dynamic_index_in_dim(up_weight, anchor, 0, keepdims=False)
        down_rows = lax.dynamic_index_in_dim(down_weight, anchor, 0, keepdims=False)
        chosen = flat_targets == group
        found = jnp.nonzero(chosen, size=slots, fill_value=0)[0].astype(jnp.int32)
        live = places < jnp.sum(chosen.astype(jnp.int32))
        owners = (found // TOP).astype(jnp.int32)
        result = run_expert(tokens[owners], gate_cols, up_cols, down_rows).astype(jnp.float32)
        scale = jnp.where(live, flat_mixing[found], 0.0)
        return total.at[owners].add(result * scale[:, None]), None

    start = jnp.zeros((TOKENS, D), jnp.float32)
    total, unused = lax.scan(visit, start, jnp.arange(N_DP, dtype=jnp.int32))
    return total.astype(jnp.bfloat16)
```

```python
import functools

import jax
import jax.numpy as jnp
from jax import lax
from jax.experimental import pallas as pl
from jax.experimental.pallas import tpu as pltpu
from jax.sharding import PartitionSpec as P

MESH = pl.DeviceIdType.MESH
F32, BF16 = jnp.float32, jnp.bfloat16
PLANE, LINE = 4, 4


def share_of(targets, mixing, move_plan, lanes):
    anchors = jnp.sum(
        jnp.where(targets[:, :, None] == lanes, move_plan[None, None, :], 0), axis=2
    )
    return jnp.sum(jnp.where(anchors[:, :, None] == lanes, mixing[:, :, None], 0.0), axis=1)


def tile_of(extent, largest):
    return next(t for t in (512, 256, 128) if t <= largest and extent % t == 0)


GATHER_Z, SUM_Z = (1,), (1, 2)
PIECES = 2
ORDER = (
    "start", "sa", "hfx.0", "hfy.0", "c1.2", "dz", "c1.1", "pa.0", "hfy.2", "hfx.2",
    "pb.0", "hi.0", "c1.3", "c2.1", "pa.1", "pb.1", "hi.1", "pa.2", "pb.2", "hi.2",
    "hfx.3", "hfy.3", "lo.1.0", "lo.2.0", "lo.2.1", "pa.3", "pb.3", "hi.3", "lo.1.1", "lo.3.0",
    "rs.1.0", "lo.3.1", "rs.2.1", "lo.0.0", "zdr.2.1", "rfx.3.0", "rfy.3.0", "zdr.2.0", "rs.2.0", "lo.0.1",
    "rfx.3.1", "rfy.3.1", "rs.3.0", "dd.0.1", "zr.2.1", "dd.0.0", "rs.3.1", "rs.1.1", "zr.2.0", "rfy.0.1",
    "rfx.0.1", "zr.3.0", "rfy.0.0", "rfx.0.0", "rs.0.1", "zr.3.1", "rs.0.0", "fi.1", "fi.0",
)


def pieces_of(wide, tile):
    tiles = wide // tile
    cuts = [-(-tiles * c // PIECES) * tile for c in range(PIECES + 1)]
    return [(a, b - a) for a, b in zip(cuts[:-1], cuts[1:])]


def kernel(
    groups, tokens, targets, mixing, plan, gate_hbm, up_hbm, down_hbm, out,
    gate, up, down, tok, psend, precv, pown, hid, cont, dsend, dland,
    xsend, ysend, xland, yland, zsend, zland, vsend, vland, acc,
    wsem, own_sem, ag_s, ag_r, col_s, col_r, ep_s, ep_r, d_s, d_r, xy_s, xy_r, z_s, z_r, v_s, v_r,
):
    me = lax.axis_index("dp")
    core = lax.axis_index("ep")
    rows, wide = tokens.shape
    half = rows // 2
    keep = psend.shape[2] // 2
    block = PLANE * rows
    z = me // PLANE
    j = me % PLANE
    y, x = j // 2, j % 2
    jx, jy, jd = y * 2 + 1 - x, (1 - y) * 2 + x, (1 - y) * 2 + 1 - x
    top = z // 2
    inner = z + top * (LINE - 1 - 2 * z)
    mirrored = (inner, 1 - inner, 2, 3)
    plane = [q + top * (LINE - 1 - 2 * q) for q in mirrored]
    X, Y, E = {"dp": z * PLANE + jx}, {"dp": z * PLANE + jy}, {"ep": 1 - core}
    PARTNER, ACROSS = {"dp": plane[1] * PLANE + j}, {"dp": plane[2] * PLANE + j}

    def at_rows(slot):
        return pl.ds(pl.multiple_of(slot * rows, rows), rows)

    def at_half(slot, h):
        return pl.ds(pl.multiple_of(slot * rows + h * half, half), half)

    def token_block(s, q):
        return tok.at[at_rows(plane[s] * PLANE + q)]

    def token_half(s, q, h):
        return tok.at[at_half(plane[s] * PLANE + q, h)]

    weight_copies = [
        pltpu.make_async_copy(gate_hbm, gate, wsem.at[0]),
        pltpu.make_async_copy(up_hbm, up, wsem.at[1]),
        pltpu.make_async_copy(down_hbm, down, wsem.at[2]),
    ]
    own_copy = pltpu.make_async_copy(tokens, tok.at[at_rows(me), pl.ds(0, wide)], own_sem.at[0])
    own_copy.start()

    barrier = pltpu.get_barrier_semaphore()
    for device in (X, Y, E, PARTNER, ACROSS):
        pl.semaphore_signal(barrier, inc=1, device_id=device, device_id_type=MESH)

    @pl.when(inner == 1)
    def _():
        pl.semaphore_signal(
            barrier, inc=1, device_id={"dp": plane[3] * PLANE + j}, device_id_type=MESH
        )

    lane = lax.broadcasted_iota(jnp.int32, (rows, tok.shape[1] - wide), 1)
    slot = lane % groups
    share = jnp.zeros(lane.shape, F32)
    for k in range(targets.shape[1]):
        hit = (lane == targets[:, pl.ds(k, 1)]) & (lane < groups)
        anchor = jnp.sum(jnp.where(hit, plan[...], 0), axis=1, keepdims=True)
        share += jnp.where(slot == anchor, mixing[:, pl.ds(k, 1)], 0.0)
    high = share.astype(BF16).astype(F32)
    middle = (share - high).astype(BF16).astype(F32)
    low = share - high - middle
    parts = jnp.where(
        lane < groups,
        high,
        jnp.where(lane < 2 * groups, middle, jnp.where(lane < 3 * groups, low, 0.0)),
    )
    tok[at_rows(me), pl.ds(wide, tok.shape[1] - wide)] = parts.astype(BF16)
    own_copy.wait()
    pl.semaphore_wait(barrier, 5 + inner)

    started, inner_started = [], []

    def copy(src, dst, ss, rs, device):
        return pltpu.make_async_remote_copy(
            src_ref=src, dst_ref=dst, send_sem=ss, recv_sem=rs,
            device_id=device, device_id_type=MESH,
        )

    def send(src, dst, ss, rs, device):
        c = copy(src, dst, ss, rs, device)
        c.start()
        started.append(c)

    def send_inner(q, s, which, slot, there, device):
        def make():
            b = token_block(s, q)
            return copy(b, b, col_s.at[which, slot], col_r.at[which, there()], device)

        pl.when(inner == 1)(lambda: make().start())
        inner_started.append(make)

    def landed(dst, rs):
        pltpu.make_async_remote_copy(
            src_ref=dst, dst_ref=dst, send_sem=rs, recv_sem=rs,
            device_id=X, device_id_type=MESH,
        ).wait_recv()

    gtile = tile_of(keep, 512)
    dtile = tile_of(wide, 512)
    pieces = pieces_of(wide, dtile)

    def cut(c):
        return pl.ds(*pieces[c])

    def spread(s):
        b = token_block(s, j)
        send(b, b, ag_s.at[0, s], ag_r.at[0, s], X)
        send(b, b, ag_s.at[1, s], ag_r.at[1, s], Y)

    def across():
        b = token_block(0, j)
        return copy(b, b, col_s.at[0, 0], col_r.at[0, 3 - inner], ACROSS)

    def sa():
        pl.when(inner == 0)(lambda: across().start())

    def start():
        b = token_block(0, j)
        pl.when(inner == 1)(lambda: across().start())
        spread(0)
        send(b, b, col_s.at[0, 1], col_r.at[0, 1], PARTNER)
        for c in weight_copies:
            c.start()

    def hfx(s):
        landed(token_block(s, jx), ag_r.at[0, s])
        b = token_half(s, jx, 0)
        send(b, b, ag_s.at[2, s], ag_r.at[2, s], Y)

    def hfy(s):
        landed(token_block(s, jy), ag_r.at[1, s])
        b = token_half(s, jy, 1)
        send(b, b, ag_s.at[3, s], ag_r.at[3, s], X)

    def relay(which, s, q):
        if s > 1:
            send_inner(q, s, which, s, lambda: s, PARTNER)

    def c1(s):
        b = token_block(s, j)
        landed(b, col_r.at[0, s])
        relay(0, s, j)
        spread(s)

    def diag(s):
        landed(token_half(s, jd, 0), ag_r.at[2, s])
        landed(token_half(s, jd, 1), ag_r.at[3, s])

    def dz():
        diag(0)
        b = token_block(0, jd)

        if 3 in GATHER_Z:
            send(b, b, col_s.at[1, 0], col_r.at[1, 3 - inner], ACROSS)
        elif 2 in GATHER_Z:
            send_inner(jd, 0, 1, 0, lambda: 2, ACROSS)
        if 1 in GATHER_Z:
            send(b, b, col_s.at[1, 1], col_r.at[1, 1], PARTNER)

    def c2(s):
        b = token_block(s, jd)
        landed(b, col_r.at[1, s])
        relay(1, s, jd)

    def project(s, side, put):
        here = pl.ds(pl.multiple_of(plane[s] * block, block), block)

        @pl.loop(0, keep // gtile)
        def _(n):
            off = pl.multiple_of(n * gtile, gtile)
            src = pl.ds(pl.multiple_of(side * keep + off, gtile), gtile)
            lhs = tok[here, pl.ds(0, wide)]
            put[:, pl.ds(off, gtile)] = jnp.dot(lhs, gate[:, src], preferred_element_type=F32)
            put[:, pl.ds(pl.multiple_of(keep + off, gtile), gtile)] = jnp.dot(
                lhs, up[:, src], preferred_element_type=F32
            )

    loaded = set()

    def load(*which):
        for w in which:
            if w not in loaded:
                weight_copies[w].wait()
                loaded.add(w)

    def pa(s):
        if not (s in GATHER_Z or s == 0 and GATHER_Z):
            diag(s)
        if s in GATHER_Z:
            landed(token_block(s, jx), ag_r.at[0, s])
            landed(token_block(s, jy), ag_r.at[1, s])
        load(0, 1)
        project(s, 1 - core, psend.at[s])
        send(psend.at[s], precv.at[s], ep_s.at[0, s], ep_r.at[0, s], E)

    def pb(s):
        project(s, core, pown)

    def hi(s):
        landed(precv.at[s], ep_r.at[0, s])
        g = pown[:, pl.ds(0, keep)] + precv[s, :, pl.ds(0, keep)]
        u = pown[:, pl.ds(keep, keep)] + precv[s, :, pl.ds(keep, keep)]
        hid[s, core] = (g / (1.0 + jnp.exp(-g)) * u).astype(BF16)
        send(hid.at[s, core], hid.at[s, core], ep_s.at[1, s], ep_r.at[1, s], E)

    def diag_out(s, c):
        for h, k, device in ((0, 0, Y), (1, 1, X)):
            b = pl.ds(h * half, half)
            send(
                dsend.at[s, b, cut(c)], dland.at[s, b, cut(c)],
                d_s.at[k, s, c], d_r.at[k, s, c], device,
            )

    def lo(s, c):
        load(2)
        if c == 0:
            landed(hid.at[s, 1 - core], ep_r.at[1, s])
        here = pl.ds(pl.multiple_of(plane[s] * block, block), block)
        packed = tok[here, pl.ds(wide, tok.shape[1] - wide)].astype(F32)
        at = lax.broadcasted_iota(jnp.int32, packed.shape, 1)
        scale = jnp.sum(jnp.where(at % groups == me, packed, 0.0), axis=1, keepdims=True)
        first, width = pieces[c]

        @pl.loop(0, width // dtile)
        def _(n):
            cols = pl.ds(pl.multiple_of(first + n * dtile, dtile), dtile)
            e = jnp.dot(hid[s, 0], down[pl.ds(0, keep), cols], preferred_element_type=F32)
            e += jnp.dot(hid[s, 1], down[pl.ds(keep, keep), cols], preferred_element_type=F32)
            cont[s, :, cols] = e.astype(BF16).astype(F32) * scale

        if s in SUM_Z:
            xsend[s, :, cut(c)] = cont[s, at_rows(jx), cut(c)].astype(BF16)
            send(xsend.at[s, :, cut(c)], xland.at[s, :, cut(c)], xy_s.at[0, s, c], xy_r.at[0, s, c], X)
            ysend[s, :, cut(c)] = cont[s, at_rows(jy), cut(c)].astype(BF16)
            send(ysend.at[s, :, cut(c)], yland.at[s, :, cut(c)], xy_s.at[1, s, c], xy_r.at[1, s, c], Y)
            if s == 1:
                along(cont[s, at_rows(jd), cut(c)], s, c, vsend, vland, v_s, v_r)
        elif s:
            dsend[s, :, cut(c)] = cont[s, at_rows(jd), cut(c)].astype(BF16)
            diag_out(s, c)

    def along(value, s, c, put, land, ss, rs):
        put[s, :, cut(c)] = value.astype(BF16)
        if s == 1:
            device, there = plane[1], 0
        else:
            device, there = inner * plane[s] + (1 - inner) * plane[1], inner + (1 - inner) * s
        send(
            put.at[s, :, cut(c)], land.at[there, :, cut(c)],
            ss.at[s, c], rs.at[there, c], {"dp": device * PLANE + j},
        )

    def add_partner(ref, s, c, land, rs):
        @pl.when(inner == 1)
        def _():
            landed(land.at[s, :, cut(c)], rs.at[s, c])
            ref[:, cut(c)] += land[s, :, cut(c)].astype(F32)

    def zdr(s, c):
        ref = cont.at[s, at_rows(jd)]
        add_partner(ref, s, c, vland, v_r)
        along(ref[:, cut(c)], s, c, vsend, vland, v_s, v_r)

    def dd(s, c):
        ref = cont.at[s, at_rows(jd)]
        if 1 in SUM_Z:
            landed(vland.at[0, :, cut(c)], v_r.at[0, c])
            ref[:, cut(c)] += vland[0, :, cut(c)].astype(F32)

        def from_across():
            landed(vland.at[1, :, cut(c)], v_r.at[1, c])
            ref[:, cut(c)] += vland[1, :, cut(c)].astype(F32)

        if 2 in SUM_Z and 3 in SUM_Z:
            from_across()
        elif 2 in SUM_Z:
            pl.when(inner == 1)(from_across)
        dsend[s, :, cut(c)] = ref[:, cut(c)].astype(BF16)
        diag_out(s, c)

    def rfx(s, c):
        b = pl.ds(0, half)
        landed(dland.at[s, b, cut(c)], d_r.at[0, s, c])
        xsend[s, b, cut(c)] = (
            cont[s, at_half(jx, 0), cut(c)] + dland[s, b, cut(c)].astype(F32)
        ).astype(BF16)
        xsend[s, pl.ds(half, half), cut(c)] = cont[s, at_half(jx, 1), cut(c)].astype(BF16)
        send(xsend.at[s, :, cut(c)], xland.at[s, :, cut(c)], xy_s.at[0, s, c], xy_r.at[0, s, c], X)

    def rfy(s, c):
        b = pl.ds(half, half)
        landed(dland.at[s, b, cut(c)], d_r.at[1, s, c])
        ysend[s, pl.ds(0, half), cut(c)] = cont[s, at_half(jy, 0), cut(c)].astype(BF16)
        ysend[s, b, cut(c)] = (
            cont[s, at_half(jy, 1), cut(c)] + dland[s, b, cut(c)].astype(F32)
        ).astype(BF16)
        send(ysend.at[s, :, cut(c)], yland.at[s, :, cut(c)], xy_s.at[1, s, c], xy_r.at[1, s, c], Y)

    def rs(s, c):
        landed(xland.at[s, :, cut(c)], xy_r.at[0, s, c])
        landed(yland.at[s, :, cut(c)], xy_r.at[1, s, c])
        total = (
            cont[s, at_rows(j), cut(c)]
            + xland[s, :, cut(c)].astype(F32)
            + yland[s, :, cut(c)].astype(F32)
        )
        if s == 1:
            along(total, s, c, zsend, zland, z_s, z_r)
        else:
            acc[s, :, cut(c)] = total

    def zr(s, c):
        add_partner(acc.at[s], s, c, zland, z_r)
        along(acc[s, :, cut(c)], s, c, zsend, zland, z_s, z_r)

    def fi(c):
        total = acc[0, :, cut(c)]
        for slot in range(2):
            landed(zland.at[slot, :, cut(c)], z_r.at[slot, c])
            total += zland[slot, :, cut(c)].astype(F32)
        out[:, cut(c)] = total.astype(BF16)

    steps = {
        "start": start, "sa": sa, "hfx": hfx, "hfy": hfy, "c1": c1, "c2": c2, "dz": dz, "pa": pa, "pb": pb,
        "hi": hi, "lo": lo, "zdr": zdr, "dd": dd, "rfx": rfx, "rfy": rfy, "rs": rs, "zr": zr, "fi": fi,
    }
    for step in ORDER:
        name, *at = step.split(".")
        steps[name](*map(int, at))

    for c in started + [across()]:
        c.wait_send()

    @pl.when(inner == 1)
    def _():
        for make in inner_started:
            make().wait_send()


def fused(tokens, gate_weight, up_weight, down_weight, targets, mixing, move_plan):
    groups = lax.axis_size("dp")
    rows, wide = tokens.shape
    lanes = -(-3 * groups // 128) * 128
    plan = jnp.pad(move_plan[None], ((0, 0), (0, lanes - groups)))
    full = gate_weight.shape[2]
    keep = full // lax.axis_size("ep")
    block = PLANE * rows
    VM, DMA = pltpu.VMEM, pltpu.SemaphoreType.DMA
    slots = VM((LINE, rows, wide), BF16)
    return pl.pallas_call(
        functools.partial(kernel, groups),
        out_shape=jax.ShapeDtypeStruct((rows, wide), BF16),
        in_specs=[pl.BlockSpec(memory_space=pl.ANY)]
        + [pl.BlockSpec(memory_space=pltpu.VMEM)] * 3
        + [pl.BlockSpec(memory_space=pl.ANY)] * 3,
        out_specs=pl.BlockSpec(memory_space=pltpu.VMEM),
        scratch_shapes=[
            VM((wide, full), BF16), VM((wide, full), BF16), VM((full, wide), BF16),
            VM((groups * rows, wide + lanes), BF16),
            VM((LINE, block, 2 * keep), F32), VM((LINE, block, 2 * keep), F32),
            VM((block, 2 * keep), F32), VM((LINE, 2, block, keep), BF16),
            VM((LINE, block, wide), F32),
            slots, slots, slots, slots, slots, slots, slots, slots, slots, slots,
            VM((LINE, rows, wide), F32),
            DMA((3,)), DMA((1,)), DMA((4, LINE)), DMA((4, LINE)), DMA((2, LINE)), DMA((2, LINE)),
            DMA((2, LINE)), DMA((2, LINE)), DMA((2, LINE, PIECES)), DMA((2, LINE, PIECES)),
            DMA((2, LINE, PIECES)), DMA((2, LINE, PIECES)), DMA((LINE, PIECES)), DMA((LINE, PIECES)),
            DMA((LINE, PIECES)), DMA((LINE, PIECES)),
        ],
        compiler_params=pltpu.CompilerParams(
            collective_id=0, has_side_effects=True, vmem_limit_bytes=50 * 1024 * 1024
        ),
    )(tokens, targets, mixing, plan, gate_weight[0], up_weight[0], down_weight[0])


def plain(tokens, gate_weight, up_weight, down_weight, targets, mixing, move_plan):
    groups = lax.axis_size("dp")
    me = lax.axis_index("dp")
    lanes = jnp.arange(groups, dtype=jnp.int32)
    share = share_of(targets, mixing, move_plan, lanes)
    shares = lax.all_gather(share, "dp", axis=0, tiled=True)
    rows = lax.all_gather(tokens, "dp", axis=0, tiled=True)
    width = rows.shape[0]
    dims = (((0,), (1,)), ((), ()))
    gate_term = lax.dot_general(gate_weight[0], rows, dims, preferred_element_type=F32)
    up_term = lax.dot_general(up_weight[0], rows, dims, preferred_element_type=F32)
    summed = lax.psum_scatter(
        jnp.concatenate([gate_term, up_term], axis=1), "ep", scatter_dimension=0, tiled=True
    )
    hidden = (jax.nn.silu(summed[:, :width]) * summed[:, width:]).astype(BF16)
    output = lax.dot_general(
        lax.all_gather(hidden, "ep", axis=0, tiled=True),
        down_weight[0],
        (((0,), (0,)), ((), ())),
        preferred_element_type=F32,
    )
    scale = jnp.sum(jnp.where(lanes == me, shares, 0.0), axis=1, keepdims=True)
    scaled = output.astype(BF16).astype(F32) * scale
    return lax.psum_scatter(scaled.astype(BF16), "dp", scatter_dimension=0, tiled=True)


def solution(mesh):
    small = mesh.shape["dp"] == PLANE * LINE and mesh.shape["ep"] == 2
    return jax.shard_map(
        fused if small else plain,
        mesh=mesh,
        in_specs=(
            P("dp", "ep"),
            P("dp", "ep", None),
            P("dp", "ep", None),
            P("dp", None, "ep"),
            P("dp", None),
            P("dp", None),
            P(),
        ),
        out_specs=P("dp", "ep"),
        check_vma=False,
    )
```

```python
import functools

import jax
import jax.numpy as jnp
from jax import lax
from jax.experimental import pallas as pl
from jax.experimental.pallas import tpu as pltpu
from jax.sharding import PartitionSpec as P

MESH = pl.DeviceIdType.MESH
F32, BF16 = jnp.float32, jnp.bfloat16
PLANE, LINE = 4, 4


def share_of(targets, mixing, move_plan, lanes):
    anchors = jnp.sum(
        jnp.where(targets[:, :, None] == lanes, move_plan[None, None, :], 0), axis=2
    )
    return jnp.sum(jnp.where(anchors[:, :, None] == lanes, mixing[:, :, None], 0.0), axis=1)


def tile_of(extent, largest):
    return next(t for t in (512, 256, 128) if t <= largest and extent % t == 0)


GATHER_Z, SUM_Z = (1,), (1, 2)
PIECES = 2
ORDER = (
    "start", "sa", "hfx.0", "hfy.0", "c1.2", "dz", "c1.1", "pa.0", "hfy.2", "hfx.2",
    "pb.0", "hi.0", "c1.3", "c2.1", "pa.1", "pb.1", "hi.1", "pa.2", "pb.2", "hi.2",
    "hfx.3", "hfy.3", "lo.2.0", "lo.2.1", "lo.1.0", "pa.3", "pb.3", "hi.3", "lo.1.1", "lo.3.0",
    "lo.3.1", "rs.2.0", "rs.2.1", "zdr.2.0", "zdr.2.1", "rs.1.0", "rs.1.1", "rfx.3.0", "rfy.3.0", "rfx.3.1",
    "rfy.3.1", "lo.0.0", "zr.2.0", "dd.0.0", "lo.0.1", "zr.2.1", "dd.0.1", "rs.3.0", "rs.3.1", "zr.3.0",
    "rfy.0.0", "rfx.0.0", "zr.3.1", "rfy.0.1", "rfx.0.1", "rs.0.0", "fi.0", "rs.0.1", "fi.1",
)


def pieces_of(wide, tile):
    tiles = wide // tile
    cuts = [-(-tiles * c // PIECES) * tile for c in range(PIECES + 1)]
    return [(a, b - a) for a, b in zip(cuts[:-1], cuts[1:])]


def kernel(
    groups, tokens, targets_hbm, mixing_hbm, plan_hbm, gate_hbm, up_hbm, down_hbm, out,
    targets, mixing, plan, gate, up, down, tok, psend, precv, pown, hid, cont, dsend, dland,
    xsend, ysend, xland, yland, zsend, zland, vsend, vland, acc,
    wsem, own_sem, ag_s, ag_r, col_s, col_r, ep_s, ep_r, d_s, d_r, xy_s, xy_r, z_s, z_r, v_s, v_r,
):
    me = lax.axis_index("dp")
    core = lax.axis_index("ep")
    rows, wide = tokens.shape
    half = rows // 2
    keep = psend.shape[2] // 2
    block = PLANE * rows
    z = me // PLANE
    j = me % PLANE
    y, x = j // 2, j % 2
    jx, jy, jd = y * 2 + 1 - x, (1 - y) * 2 + x, (1 - y) * 2 + 1 - x
    top = z // 2
    inner = z + top * (LINE - 1 - 2 * z)
    mirrored = (inner, 1 - inner, 2, 3)
    plane = [q + top * (LINE - 1 - 2 * q) for q in mirrored]
    X, Y, E = {"dp": z * PLANE + jx}, {"dp": z * PLANE + jy}, {"ep": 1 - core}
    PARTNER, ACROSS = {"dp": plane[1] * PLANE + j}, {"dp": plane[2] * PLANE + j}

    def at_rows(slot):
        return pl.ds(pl.multiple_of(slot * rows, rows), rows)

    def at_half(slot, h):
        return pl.ds(pl.multiple_of(slot * rows + h * half, half), half)

    def token_block(s, q):
        return tok.at[at_rows(plane[s] * PLANE + q)]

    def token_half(s, q, h):
        return tok.at[at_half(plane[s] * PLANE + q, h)]

    weight_copies = [
        pltpu.make_async_copy(gate_hbm, gate, wsem.at[0]),
        pltpu.make_async_copy(up_hbm, up, wsem.at[1]),
        pltpu.make_async_copy(down_hbm, down, wsem.at[2]),
    ]
    own_copy = pltpu.make_async_copy(tokens, tok.at[at_rows(me), pl.ds(0, wide)], own_sem.at[0])
    own_copy.start()

    barrier = pltpu.get_barrier_semaphore()
    for device in (X, Y, E, PARTNER, ACROSS):
        pl.semaphore_signal(barrier, inc=1, device_id=device, device_id_type=MESH)

    @pl.when(inner == 1)
    def _():
        pl.semaphore_signal(
            barrier, inc=1, device_id={"dp": plane[3] * PLANE + j}, device_id_type=MESH
        )

    small_copies = [
        pltpu.make_async_copy(targets_hbm, targets, own_sem.at[1]),
        pltpu.make_async_copy(mixing_hbm, mixing, own_sem.at[2]),
        pltpu.make_async_copy(plan_hbm, plan, own_sem.at[3]),
    ]
    for c in small_copies:
        c.start()
    for c in small_copies:
        c.wait()
    named, moved = targets[...], plan[...]
    anchor = jnp.zeros(named.shape, jnp.int32)
    for e in range(groups):
        anchor = jnp.where(named == e, moved[:, e:e + 1], anchor)
    lanes = tok.shape[1] - wide
    lane = lax.broadcasted_iota(jnp.int32, (rows, lanes), 1)
    slot = lax.broadcasted_iota(jnp.int32, (lanes, rows), 0) % groups
    share = jnp.zeros(slot.shape, F32)
    for k in range(named.shape[0]):
        share += jnp.where(slot == anchor[k:k + 1, :], mixing[k:k + 1, :], 0.0)
    share = share.T
    high = share.astype(BF16).astype(F32)
    middle = (share - high).astype(BF16).astype(F32)
    low = share - high - middle
    parts = jnp.where(
        lane < groups,
        high,
        jnp.where(lane < 2 * groups, middle, jnp.where(lane < 3 * groups, low, 0.0)),
    )
    tok[at_rows(me), pl.ds(wide, tok.shape[1] - wide)] = parts.astype(BF16)
    own_copy.wait()
    pl.semaphore_wait(barrier, 5 + inner)

    started, inner_started = [], []

    def copy(src, dst, ss, rs, device):
        return pltpu.make_async_remote_copy(
            src_ref=src, dst_ref=dst, send_sem=ss, recv_sem=rs,
            device_id=device, device_id_type=MESH,
        )

    def send(src, dst, ss, rs, device):
        c = copy(src, dst, ss, rs, device)
        c.start()
        started.append(c)

    def send_inner(q, s, which, slot, there, device):
        def make():
            b = token_block(s, q)
            return copy(b, b, col_s.at[which, slot], col_r.at[which, there()], device)

        pl.when(inner == 1)(lambda: make().start())
        inner_started.append(make)

    def landed(dst, rs):
        pltpu.make_async_remote_copy(
            src_ref=dst, dst_ref=dst, send_sem=rs, recv_sem=rs,
            device_id=X, device_id_type=MESH,
        ).wait_recv()

    gtile = tile_of(keep, 512)
    dtile = tile_of(wide, 512)
    pieces = pieces_of(wide, dtile)

    def cut(c):
        return pl.ds(*pieces[c])

    def spread(s):
        b = token_block(s, j)
        send(b, b, ag_s.at[0, s], ag_r.at[0, s], X)
        send(b, b, ag_s.at[1, s], ag_r.at[1, s], Y)

    def across():
        b = token_block(0, j)
        return copy(b, b, col_s.at[0, 0], col_r.at[0, 3 - inner], ACROSS)

    def sa():
        pl.when(inner == 0)(lambda: across().start())

    def start():
        b = token_block(0, j)
        pl.when(inner == 1)(lambda: across().start())
        spread(0)
        send(b, b, col_s.at[0, 1], col_r.at[0, 1], PARTNER)
        for c in weight_copies:
            c.start()

    def hfx(s):
        landed(token_block(s, jx), ag_r.at[0, s])
        b = token_half(s, jx, 0)
        send(b, b, ag_s.at[2, s], ag_r.at[2, s], Y)

    def hfy(s):
        landed(token_block(s, jy), ag_r.at[1, s])
        b = token_half(s, jy, 1)
        send(b, b, ag_s.at[3, s], ag_r.at[3, s], X)

    def relay(which, s, q):
        if s > 1:
            send_inner(q, s, which, s, lambda: s, PARTNER)

    def c1(s):
        b = token_block(s, j)
        landed(b, col_r.at[0, s])
        relay(0, s, j)
        spread(s)

    def diag(s):
        landed(token_half(s, jd, 0), ag_r.at[2, s])
        landed(token_half(s, jd, 1), ag_r.at[3, s])

    def dz():
        diag(0)
        b = token_block(0, jd)

        if 3 in GATHER_Z:
            send(b, b, col_s.at[1, 0], col_r.at[1, 3 - inner], ACROSS)
        elif 2 in GATHER_Z:
            send_inner(jd, 0, 1, 0, lambda: 2, ACROSS)
        if 1 in GATHER_Z:
            send(b, b, col_s.at[1, 1], col_r.at[1, 1], PARTNER)

    def c2(s):
        b = token_block(s, jd)
        landed(b, col_r.at[1, s])
        relay(1, s, jd)

    def project(s, side, put):
        here = pl.ds(pl.multiple_of(plane[s] * block, block), block)

        @pl.loop(0, keep // gtile)
        def _(n):
            off = pl.multiple_of(n * gtile, gtile)
            src = pl.ds(pl.multiple_of(side * keep + off, gtile), gtile)
            lhs = tok[here, pl.ds(0, wide)]
            put[:, pl.ds(off, gtile)] = jnp.dot(lhs, gate[:, src], preferred_element_type=F32)
            put[:, pl.ds(pl.multiple_of(keep + off, gtile), gtile)] = jnp.dot(
                lhs, up[:, src], preferred_element_type=F32
            )

    loaded = set()

    def load(*which):
        for w in which:
            if w not in loaded:
                weight_copies[w].wait()
                loaded.add(w)

    def pa(s):
        if not (s in GATHER_Z or s == 0 and GATHER_Z):
            diag(s)
        if s in GATHER_Z:
            landed(token_block(s, jx), ag_r.at[0, s])
            landed(token_block(s, jy), ag_r.at[1, s])
        load(0, 1)
        project(s, 1 - core, psend.at[s])
        send(psend.at[s], precv.at[s], ep_s.at[0, s], ep_r.at[0, s], E)

    def pb(s):
        project(s, core, pown)

    def hi(s):
        landed(precv.at[s], ep_r.at[0, s])
        g = pown[:, pl.ds(0, keep)] + precv[s, :, pl.ds(0, keep)]
        u = pown[:, pl.ds(keep, keep)] + precv[s, :, pl.ds(keep, keep)]
        hid[s, core] = (g / (1.0 + jnp.exp(-g)) * u).astype(BF16)
        send(hid.at[s, core], hid.at[s, core], ep_s.at[1, s], ep_r.at[1, s], E)

    def diag_out(s, c):
        for h, k, device in ((0, 0, Y), (1, 1, X)):
            b = pl.ds(h * half, half)
            send(
                dsend.at[s, b, cut(c)], dland.at[s, b, cut(c)],
                d_s.at[k, s, c], d_r.at[k, s, c], device,
            )

    def lo(s, c):
        load(2)
        if c == 0:
            landed(hid.at[s, 1 - core], ep_r.at[1, s])
        here = pl.ds(pl.multiple_of(plane[s] * block, block), block)
        packed = tok[here, pl.ds(wide, tok.shape[1] - wide)].astype(F32)
        at = lax.broadcasted_iota(jnp.int32, packed.shape, 1)
        scale = jnp.sum(jnp.where(at % groups == me, packed, 0.0), axis=1, keepdims=True)
        first, width = pieces[c]

        @pl.loop(0, width // dtile)
        def _(n):
            cols = pl.ds(pl.multiple_of(first + n * dtile, dtile), dtile)
            e = jnp.dot(hid[s, 0], down[pl.ds(0, keep), cols], preferred_element_type=F32)
            e += jnp.dot(hid[s, 1], down[pl.ds(keep, keep), cols], preferred_element_type=F32)
            cont[s, :, cols] = e.astype(BF16).astype(F32) * scale

        if s in SUM_Z:
            xsend[s, :, cut(c)] = cont[s, at_rows(jx), cut(c)].astype(BF16)
            send(xsend.at[s, :, cut(c)], xland.at[s, :, cut(c)], xy_s.at[0, s, c], xy_r.at[0, s, c], X)
            ysend[s, :, cut(c)] = cont[s, at_rows(jy), cut(c)].astype(BF16)
            send(ysend.at[s, :, cut(c)], yland.at[s, :, cut(c)], xy_s.at[1, s, c], xy_r.at[1, s, c], Y)
            if s == 1:
                along(cont[s, at_rows(jd), cut(c)], s, c, vsend, vland, v_s, v_r)
        elif s:
            dsend[s, :, cut(c)] = cont[s, at_rows(jd), cut(c)].astype(BF16)
            diag_out(s, c)

    def along(value, s, c, put, land, ss, rs):
        put[s, :, cut(c)] = value.astype(BF16)
        if s == 1:
            device, there = plane[1], 0
        else:
            device, there = inner * plane[s] + (1 - inner) * plane[1], inner + (1 - inner) * s
        send(
            put.at[s, :, cut(c)], land.at[there, :, cut(c)],
            ss.at[s, c], rs.at[there, c], {"dp": device * PLANE + j},
        )

    def add_partner(ref, s, c, land, rs):
        @pl.when(inner == 1)
        def _():
            landed(land.at[s, :, cut(c)], rs.at[s, c])
            ref[:, cut(c)] += land[s, :, cut(c)].astype(F32)

    def zdr(s, c):
        ref = cont.at[s, at_rows(jd)]
        add_partner(ref, s, c, vland, v_r)
        along(ref[:, cut(c)], s, c, vsend, vland, v_s, v_r)

    def dd(s, c):
        ref = cont.at[s, at_rows(jd)]
        if 1 in SUM_Z:
            landed(vland.at[0, :, cut(c)], v_r.at[0, c])
            ref[:, cut(c)] += vland[0, :, cut(c)].astype(F32)

        def from_across():
            landed(vland.at[1, :, cut(c)], v_r.at[1, c])
            ref[:, cut(c)] += vland[1, :, cut(c)].astype(F32)

        if 2 in SUM_Z and 3 in SUM_Z:
            from_across()
        elif 2 in SUM_Z:
            pl.when(inner == 1)(from_across)
        dsend[s, :, cut(c)] = ref[:, cut(c)].astype(BF16)
        diag_out(s, c)

    def rfx(s, c):
        b = pl.ds(0, half)
        landed(dland.at[s, b, cut(c)], d_r.at[0, s, c])
        xsend[s, b, cut(c)] = (
            cont[s, at_half(jx, 0), cut(c)] + dland[s, b, cut(c)].astype(F32)
        ).astype(BF16)
        xsend[s, pl.ds(half, half), cut(c)] = cont[s, at_half(jx, 1), cut(c)].astype(BF16)
        send(xsend.at[s, :, cut(c)], xland.at[s, :, cut(c)], xy_s.at[0, s, c], xy_r.at[0, s, c], X)

    def rfy(s, c):
        b = pl.ds(half, half)
        landed(dland.at[s, b, cut(c)], d_r.at[1, s, c])
        ysend[s, pl.ds(0, half), cut(c)] = cont[s, at_half(jy, 0), cut(c)].astype(BF16)
        ysend[s, b, cut(c)] = (
            cont[s, at_half(jy, 1), cut(c)] + dland[s, b, cut(c)].astype(F32)
        ).astype(BF16)
        send(ysend.at[s, :, cut(c)], yland.at[s, :, cut(c)], xy_s.at[1, s, c], xy_r.at[1, s, c], Y)

    def rs(s, c):
        landed(xland.at[s, :, cut(c)], xy_r.at[0, s, c])
        landed(yland.at[s, :, cut(c)], xy_r.at[1, s, c])
        total = (
            cont[s, at_rows(j), cut(c)]
            + xland[s, :, cut(c)].astype(F32)
            + yland[s, :, cut(c)].astype(F32)
        )
        if s == 1:
            along(total, s, c, zsend, zland, z_s, z_r)
        else:
            acc[s, :, cut(c)] = total

    def zr(s, c):
        add_partner(acc.at[s], s, c, zland, z_r)
        along(acc[s, :, cut(c)], s, c, zsend, zland, z_s, z_r)

    def fi(c):
        total = acc[0, :, cut(c)]
        for slot in range(2):
            landed(zland.at[slot, :, cut(c)], z_r.at[slot, c])
            total += zland[slot, :, cut(c)].astype(F32)
        out[:, cut(c)] = total.astype(BF16)

    steps = {
        "start": start, "sa": sa, "hfx": hfx, "hfy": hfy, "c1": c1, "c2": c2, "dz": dz, "pa": pa, "pb": pb,
        "hi": hi, "lo": lo, "zdr": zdr, "dd": dd, "rfx": rfx, "rfy": rfy, "rs": rs, "zr": zr, "fi": fi,
    }
    for step in ORDER:
        name, *at = step.split(".")
        steps[name](*map(int, at))

    for c in started + [across()]:
        c.wait_send()

    @pl.when(inner == 1)
    def _():
        for make in inner_started:
            make().wait_send()


def fused(tokens, gate_weight, up_weight, down_weight, targets, mixing, move_plan):
    groups = lax.axis_size("dp")
    rows, wide = tokens.shape
    lanes = -(-3 * groups // 128) * 128
    full = gate_weight.shape[2]
    keep = full // lax.axis_size("ep")
    block = PLANE * rows
    VM, DMA = pltpu.VMEM, pltpu.SemaphoreType.DMA
    slots = VM((LINE, rows, wide), BF16)
    return pl.pallas_call(
        functools.partial(kernel, groups),
        out_shape=jax.ShapeDtypeStruct((rows, wide), BF16),
        in_specs=[pl.BlockSpec(memory_space=pltpu.HBM)] * 7,
        out_specs=pl.BlockSpec(memory_space=pltpu.VMEM),
        scratch_shapes=[
            VM(targets.T.shape, jnp.int32), VM(mixing.T.shape, F32), VM((1, groups), jnp.int32),
            VM((wide, full), BF16), VM((wide, full), BF16), VM((full, wide), BF16),
            VM((groups * rows, wide + lanes), BF16),
            VM((LINE, block, 2 * keep), F32), VM((LINE, block, 2 * keep), F32),
            VM((block, 2 * keep), F32), VM((LINE, 2, block, keep), BF16),
            VM((LINE, block, wide), F32),
            slots, slots, slots, slots, slots, slots, slots, slots, slots, slots,
            VM((LINE, rows, wide), F32),
            DMA((3,)), DMA((4,)), DMA((4, LINE)), DMA((4, LINE)), DMA((2, LINE)), DMA((2, LINE)),
            DMA((2, LINE)), DMA((2, LINE)), DMA((2, LINE, PIECES)), DMA((2, LINE, PIECES)),
            DMA((2, LINE, PIECES)), DMA((2, LINE, PIECES)), DMA((LINE, PIECES)), DMA((LINE, PIECES)),
            DMA((LINE, PIECES)), DMA((LINE, PIECES)),
        ],
        compiler_params=pltpu.CompilerParams(
            collective_id=0, has_side_effects=True, vmem_limit_bytes=54 * 1024 * 1024
        ),
    )(tokens, targets.T, mixing.T, move_plan[None], gate_weight[0], up_weight[0], down_weight[0])


def plain(tokens, gate_weight, up_weight, down_weight, targets, mixing, move_plan):
    groups = lax.axis_size("dp")
    me = lax.axis_index("dp")
    lanes = jnp.arange(groups, dtype=jnp.int32)
    share = share_of(targets, mixing, move_plan, lanes)
    shares = lax.all_gather(share, "dp", axis=0, tiled=True)
    rows = lax.all_gather(tokens, "dp", axis=0, tiled=True)
    width = rows.shape[0]
    dims = (((0,), (1,)), ((), ()))
    gate_term = lax.dot_general(gate_weight[0], rows, dims, preferred_element_type=F32)
    up_term = lax.dot_general(up_weight[0], rows, dims, preferred_element_type=F32)
    summed = lax.psum_scatter(
        jnp.concatenate([gate_term, up_term], axis=1), "ep", scatter_dimension=0, tiled=True
    )
    hidden = (jax.nn.silu(summed[:, :width]) * summed[:, width:]).astype(BF16)
    output = lax.dot_general(
        lax.all_gather(hidden, "ep", axis=0, tiled=True),
        down_weight[0],
        (((0,), (0,)), ((), ())),
        preferred_element_type=F32,
    )
    scale = jnp.sum(jnp.where(lanes == me, shares, 0.0), axis=1, keepdims=True)
    scaled = output.astype(BF16).astype(F32) * scale
    return lax.psum_scatter(scaled.astype(BF16), "dp", scatter_dimension=0, tiled=True)


def solution(mesh):
    small = mesh.shape["dp"] == PLANE * LINE and mesh.shape["ep"] == 2
    return jax.shard_map(
        fused if small else plain,
        mesh=mesh,
        in_specs=(
            P("dp", "ep"),
            P("dp", "ep", None),
            P("dp", "ep", None),
            P("dp", None, "ep"),
            P("dp", None),
            P("dp", None),
            P(),
        ),
        out_specs=P("dp", "ep"),
        check_vma=False,
    )
```
